128 devices in a mesh: gx: 16 (over x, y), gy: 8 (over z, core).
Axes of the slice: x: 4, y: 4, z: 4, core: 2. Of those that a mesh axis runs over, the one named last changes fastest.
Arguments:
- field: float32 [256, 256, 1536], P('gx', 'gy'), may hold values from -24 to 24
- kappa: float32 [256, 256, 1536], P('gx', 'gy'), may hold values from 0.02 to 0.16
- history: float32 [126, 128, 64, 128], P(None, 'gx', 'gy'), may hold values from -2400 to 2400
Outputs:
- field_next: float32 [256, 256, 1536], P('gx', 'gy')
- basis: float32 [128, 128, 64, 128], P(None, 'gx', 'gy')
- factor: float32 [128, 128], replicated
The draws below stay inside these ranges and needn't reach their ends.
All inputs are finite; a program needn't handle non-finite values.
Results may differ from the reference program's by a relative error of at most 0.00018.
Values sent between devices are 32-bit elements; how exact they have to be, the bound alone decides.
No kernel may reach another device: no remote copies, remote signals or barrier semaphores. Data moves between devices by JAX's collectives and lax.ppermute only.
A program may use at most 192 MiB of HBM per device.

```python
import math
import jax
import jax.numpy as jnp
from jax import lax

NZ = 1536
PAST = 126
NX = 256
NY = 256
NXS = 128
NYS = 64
NZS = 128


def draw_history(key, part):
    key_a, key_b = jax.random.split(key, 2)
    shape = (PAST, NXS, NYS, NZS)
    across = jnp.arange(NXS, dtype=jnp.float32) / max(NXS - 1, 1)
    row_scale = 10.0 ** across
    col_scale = 10.0 ** jax.random.uniform(key_b, (PAST,), jnp.float32)
    base = jnp.clip(jax.random.normal(key_a, shape, jnp.float32), -6.0, 6.0)
    scales = row_scale[:, None] * jnp.ones((NYS,), jnp.float32)[None, :]
    out = base * col_scale[:, None, None, None] * scales[None, :, :, None]
    return out.astype(jnp.float32)


def levels(rng, dims, cuts, smallest, high):
    factor_of = 1.0
    for axis_at, blocks in cuts:
        heights = jax.random.uniform(jax.random.fold_in(jax.random.fold_in(rng, 6), axis_at), (blocks,), jnp.float32, smallest / len(cuts), high / len(cuts))
        factor_of = factor_of * jnp.repeat(jnp.exp(heights), dims[axis_at] // blocks).reshape((-1,) + (1,) * (len(dims) - 1 - axis_at))
    return factor_of


def gaussian(key, extent, width, bound, cuts=(), kind=jnp.bfloat16):
    result = jax.random.normal(key, extent, jnp.float32) * width
    if len(cuts) > 0:
        result = levels(key, extent, cuts, -0.22, 0.18) * result
    return jnp.clip(result, min=-bound, max=bound).astype(kind)


def setup_inputs(seed: int = 0) -> dict:
    key_of = jax.random.split(jax.random.key(seed), 4)
    field = gaussian(key_of[0], (NX, NY, NZ), 4.0, 24.0, ((0, 16), (1, 8)), jnp.float32)
    kappa = jnp.clip(jnp.exp(math.log(0.16) - 2.0794415 * jax.random.uniform(key_of[1], (NX, NY, NZ), jnp.float32) ** levels(key_of[1], (NX, NY, NZ), ((0, 16), (1, 8)), -0.2, 0.2)), 0.02, 0.16)
    history = draw_history(jax.random.fold_in(key_of[3], 71), 0)
    return dict(field=field, kappa=kappa, history=history)


def advance(field_pad, kappa_pad):
    field_z = jnp.pad(field_pad, ((0, 0), (0, 0), (1, 1)))
    kappa_z = jnp.pad(kappa_pad, ((0, 0), (0, 0), (1, 1)))
    centre = field_z[1:-1, 1:-1, 1:-1]
    kcentre = kappa_z[1:-1, 1:-1, 1:-1]
    places = [(slice(2, None), slice(1, -1), slice(1, -1)), (slice(None, -2), slice(1, -1), slice(1, -1)), (slice(1, -1), slice(2, None), slice(1, -1)), (slice(1, -1), slice(None, -2), slice(1, -1)), (slice(1, -1), slice(1, -1), slice(2, None)), (slice(1, -1), slice(1, -1), slice(None, -2))]
    change = jnp.zeros_like(centre)
    for place in places:
        change = change + 0.5 * (kcentre + kappa_z[place]) * (field_z[place] - centre)
    return centre + change

def sample(field):
    a, b, c = field.shape
    return field.reshape(a // 2, 2, b // 4, 4, c // 12, 12)[:, 0, :, 0, :, 0]

def reference(field, kappa, history):
    kappa_pad = jnp.pad(kappa, ((1, 1), (1, 1), (0, 0)))
    first = advance(jnp.pad(field, ((1, 1), (1, 1), (0, 0))), kappa_pad)
    second = advance(jnp.pad(first, ((1, 1), (1, 1), (0, 0))), kappa_pad)
    block = jnp.concatenate([history, sample(first)[None], sample(second)[None]], 0)
    shape = block.shape
    block = block.reshape(shape[0], -1)
    gram = jnp.einsum('ar,br->ab', block, block, precision=lax.Precision.HIGHEST) / block.shape[1]
    factor = jnp.linalg.cholesky(gram).T
    basis = lax.linalg.triangular_solve(factor.T, block, left_side=True, lower=True)
    return (second, basis.reshape(shape), factor)
```

```python
import functools

import jax
import jax.numpy as jnp
from jax import lax
from jax.experimental import pallas as pl
from jax.experimental.pallas import tpu as pltpu
from jax.sharding import PartitionSpec as P

F32, BF16 = jnp.float32, jnp.bfloat16
NT = (((1,), (1,)), ((), ()))

def split(x):
    hi = x.astype(BF16)
    return hi, (x - hi.astype(F32)).astype(BF16)

def gram_kernel(h_ref, g_ref, acc):
    i = pl.program_id(0)
    past = h_ref.shape[0]
    flat = h_ref.reshape(past * 8, 128)
    pad = jnp.zeros((128 - past, 128), F32)
    his, los = [], []
    for j in range(8):
        m = jnp.concatenate([flat[pl.ds(j, past, stride=8), :], pad], axis=0)
        hi, lo = split(m)
        his.append(hi); los.append(lo)
    hi, lo = jnp.concatenate(his, 1), jnp.concatenate(los, 1)
    both = jnp.concatenate([hi, lo], 0)
    out = lax.dot_general(hi, both, NT, preferred_element_type=F32)
    @pl.when(i == 0)
    def _(): acc[...] = out
    @pl.when(i > 0)
    def _(): acc[...] += out
    @pl.when(i == pl.num_programs(0) - 1)
    def _():
        b = acc[:, 128:]
        g_ref[...] = acc[:, :128] + b + b.T

def gram(h):
    past, rows, _ = h.shape
    return pl.pallas_call(
        gram_kernel, out_shape=jax.ShapeDtypeStruct((128, 128), F32), grid=(rows // 8,),
        in_specs=[pl.BlockSpec((past, 8, 128), lambda i: (0, i, 0))],
        out_specs=pl.BlockSpec((128, 128), lambda i: (0, 0)),
        scratch_shapes=[pltpu.VMEM((128, 256), F32)], name="gram")(h)

def basis_kernel(w_ref, h_ref, s_ref, o_ref):
    past = h_ref.shape[0]
    flat = h_ref.reshape(past * 8, 128)
    out = o_ref.reshape(128 * 8, 128)
    sf = s_ref.reshape(16, 128)
    whi, wlo = split(w_ref[...])
    lhs = jnp.concatenate([jnp.concatenate([whi, whi], 1), jnp.concatenate([wlo, wlo], 1)], 0)
    for j in range(0, 8, 2):
        ms = []
        for q in (j, j + 1):
            m = jnp.concatenate([flat[pl.ds(q, past, stride=8), :], sf[pl.ds(q, 2, stride=8), :]], axis=0)
            hi, lo = split(m)
            ms.append(jnp.concatenate([hi, lo], 0))
        r = jnp.dot(lhs, jnp.concatenate(ms, 1), preferred_element_type=F32)
        r = r[:128] + r[128:]
        out[pl.ds(j, 128, stride=8), :] = r[:, :128]
        out[pl.ds(j + 1, 128, stride=8), :] = r[:, 128:]

def basis(w, h, s):
    past, rows, _ = h.shape
    return pl.pallas_call(
        basis_kernel, out_shape=jax.ShapeDtypeStruct((128, rows, 128), F32), grid=(rows // 8,),
        in_specs=[pl.BlockSpec((128, 128), lambda i: (0, 0)), pl.BlockSpec((past, 8, 128), lambda i: (0, i, 0)),
                  pl.BlockSpec((2, 8, 128), lambda i: (0, i, 0))],
        out_specs=pl.BlockSpec((128, 8, 128), lambda i: (0, i, 0)), name="basis")(w, h, s)

def chol_kernel(g_ref, r_ref, w_ref, *, n):
    lane = lax.broadcasted_iota(jnp.int32, (8, 128), 1)
    sub = lax.broadcasted_iota(jnp.int32, (8, 128), 0)
    c = [g_ref[8 * b:8 * b + 8, :] for b in range(16)]
    for k in range(n):
        b0, s0 = k // 8, k % 8
        row = jnp.broadcast_to(c[b0][s0:s0 + 1, :], (8, 128))
        piv = jnp.broadcast_to(row[:, k:k + 1], (8, 128))
        inv = 1.0 / piv
        row = jnp.where(lane == k, 1.0, row) * inv
        for b in range(b0 if s0 < 7 else b0 + 1, 16):
            col = jnp.broadcast_to(c[b][:, k:k + 1], (8, 128))
            if b == b0:
                new = jnp.where(lane == k, 0.0, c[b]) - col * row
                c[b] = jnp.where(sub > s0, new, c[b])
            else:
                c[b] = jnp.where(lane == k, 0.0, c[b]) - col * row
    for b in range(16):
        rowi = sub + 8 * b
        d = jnp.sum(jnp.where(lane == rowi, c[b], 0.0), axis=1, keepdims=True)
        rs = 1.0 / jnp.sqrt(d)
        r_ref[8 * b:8 * b + 8, :] = jnp.where(lane >= rowi, c[b] * rs, 0.0)
        w_ref[8 * b:8 * b + 8, :] = jnp.where(lane < rowi, c[b] * rs, jnp.where(lane == rowi, rs, 0.0))

def chol(g):
    sh = jax.ShapeDtypeStruct((128, 128), F32)
    return pl.pallas_call(functools.partial(chol_kernel, n=128), out_shape=(sh, sh), name="chol")(g)

def lane_shift(x, left):
    n = x.shape[-1]
    lane = lax.broadcasted_iota(jnp.int32, x.shape, x.ndim - 1)
    if left:
        return jnp.where(lane == n - 1, 0.0, pltpu.roll(x, n - 1, x.ndim - 1))
    return jnp.where(lane == 0, 0.0, pltpu.roll(x, 1, x.ndim - 1))


def step_kernel(v_ref, k_ref, vxl, vxh, kxl, kxh, vyl, vyh, kyl, kyh, o_ref, s_ref, scr):
    nx, ny, nz = v_ref.shape
    chunk = 8

    def plane(x, vm_ref, km_ref, vp_ref, kp_ref):
        for y0 in range(0, ny, chunk):
            sl = slice(y0, y0 + chunk)
            v, k = v_ref[x, sl, :], k_ref[x, sl, :]
            acc = (k + kp_ref[sl, :]) * (vp_ref[sl, :] - v) + (k + km_ref[sl, :]) * (vm_ref[sl, :] - v)

            def up(ref, hi):
                if y0 + chunk < ny:
                    return ref[x, y0 + 1 : y0 + chunk + 1, :]
                return jnp.concatenate([ref[x, y0 + 1 : y0 + chunk, :], hi[0, pl.ds(x, 1), :]], 0)

            def down(ref, lo):
                if y0 > 0:
                    return ref[x, y0 - 1 : y0 + chunk - 1, :]
                return jnp.concatenate([lo[0, pl.ds(x, 1), :], ref[x, y0 : y0 + chunk - 1, :]], 0)

            acc += (k + up(k_ref, kyh)) * (up(v_ref, vyh) - v)
            acc += (k + down(k_ref, kyl)) * (down(v_ref, vyl) - v)
            acc += (k + lane_shift(k, True)) * (lane_shift(v, True) - v)
            acc += (k + lane_shift(k, False)) * (lane_shift(v, False) - v)
            o_ref[x, sl, :] = v + 0.5 * acc

    plane(0, vxl.at[0], kxl.at[0], v_ref.at[1], k_ref.at[1])

    def inner(x, carry):
        plane(x, v_ref.at[x - 1], k_ref.at[x - 1], v_ref.at[x + 1], k_ref.at[x + 1])
        return carry

    lax.fori_loop(1, nx - 1, inner, 0)
    plane(nx - 1, v_ref.at[nx - 2], k_ref.at[nx - 2], vxh.at[0], kxh.at[0])

    lane = lax.broadcasted_iota(jnp.int32, (8, 128), 1)

    def sampled(h, carry):
        out = jnp.zeros((8, 128), F32)
        for t in range(nz // 128):
            scr[ny * t : ny * (t + 1), :] = o_ref[2 * h, :, 128 * t : 128 * t + 128]
        for t in range(nz // 128):
            m = scr[pl.ds(ny * t, 8, stride=4), :]
            idx = 12 * lane - 128 * t
            ok = (idx >= 0) & (idx < 128)
            got = jnp.take_along_axis(m, jnp.where(ok, idx, 0), axis=1)
            out = jnp.where(ok, got, out)
        s_ref[h] = out
        return carry

    lax.fori_loop(0, nx // 2, sampled, 0)


def step(v, k, vx, kx, vy, ky):
    nx, ny, nz = v.shape
    spec = pl.BlockSpec((nx, ny, nz), lambda i: (0, 0, 0))
    xk = pl.BlockSpec((1, ny, nz), lambda i: (kx[0].shape[0] - 1, 0, 0))
    yk = pl.BlockSpec((1, nx, nz), lambda i: (ky[0].shape[0] - 1, 0, 0))
    xv = pl.BlockSpec((1, ny, nz), lambda i: (0, 0, 0))
    yv = pl.BlockSpec((1, nx, nz), lambda i: (0, 0, 0))
    return pl.pallas_call(
        step_kernel,
        out_shape=(
            jax.ShapeDtypeStruct(v.shape, F32),
            jax.ShapeDtypeStruct((nx // 2, ny // 4, nz // 12), F32),
        ),
        grid=(1,),
        in_specs=[spec, spec, xv, xv, xk, xk, yv, yv, yk, yk],
        out_specs=(spec, pl.BlockSpec((nx // 2, ny // 4, nz // 12), lambda i: (0, 0, 0))),
        scratch_shapes=[pltpu.VMEM((ny * nz // 128, 128), F32)],
        name="step",
    )(v, k, *vx, *kx, *vy, *ky)


def rows_kernel(h_ref, s1_ref, s2_ref, g_ref, o_ref, t_ref):
    i = pl.program_id(0)
    past = h_ref.shape[0]
    flat = h_ref.reshape(past * 8, 128)

    @pl.when(i == 0)
    def _():
        t_ref[...] = jnp.zeros_like(t_ref)

    t1, t2 = t_ref[0], t_ref[1]
    for j in range(8):
        a, b = s1_ref[0, j : j + 1, :], s2_ref[0, j : j + 1, :]
        m = jnp.concatenate([flat[pl.ds(j, past, stride=8), :], a, b], axis=0)
        t1 += m * a
        t2 += m * b
    t_ref[0], t_ref[1] = t1, t2

    @pl.when(i == pl.num_programs(0) - 1)
    def _():
        ones = jnp.ones((8, 128), F32)
        c1 = jnp.sum(t1, axis=1, keepdims=True)
        c2 = jnp.sum(t2, axis=1, keepdims=True)
        r1 = lax.dot_general(ones, t1, NT, precision=lax.Precision.HIGHEST, preferred_element_type=F32)
        r2 = lax.dot_general(ones, t2, NT, precision=lax.Precision.HIGHEST, preferred_element_type=F32)
        row = lax.broadcasted_iota(jnp.int32, (128, 128), 0)
        col = lax.broadcasted_iota(jnp.int32, (128, 128), 1)
        g = g_ref[...]
        g = jnp.where(col == past, c1, jnp.where(col == past + 1, c2, g))
        g = jnp.where(row == past, r1[:1], jnp.where(row == past + 1, r2[:1], g))
        o_ref[...] = g


def rows(h, s1, s2, g):
    past, n, _ = h.shape
    return pl.pallas_call(
        rows_kernel,
        out_shape=jax.ShapeDtypeStruct((128, 128), F32),
        grid=(n // 8,),
        in_specs=[
            pl.BlockSpec((past, 8, 128), lambda i: (0, i, 0)),
            pl.BlockSpec((1, 8, 128), lambda i: (i, 0, 0)),
            pl.BlockSpec((1, 8, 128), lambda i: (i, 0, 0)),
            pl.BlockSpec((128, 128), lambda i: (0, 0)),
        ],
        out_specs=pl.BlockSpec((128, 128), lambda i: (0, 0)),
        scratch_shapes=[pltpu.VMEM((2, 128, 128), F32)],
        name="rows",
    )(h, s1, s2, g)


def reversed_in(n, size, span):
    out = []
    for i in range(n):
        unit, rest = divmod(i, span)
        block, at = divmod(unit, size)
        out.append((i, (block * size + size - 1 - at) * span + rest))
    return out


def total(g):
    low = lax.axis_index("gy") % 2 == 0
    half = g.shape[0] // 2
    mine, other = jnp.where(low, g[:half], g[half:]), jnp.where(low, g[half:], g[:half])
    core = reversed_in(8, 2, 1)
    mine += lax.ppermute(other, "gy", core)
    for axis, n, span in (("gy", 8, 2), ("gx", 16, 1), ("gx", 16, 4)):
        for size in (2, 4):
            mine += lax.ppermute(mine, axis, reversed_in(n, size, span))
    other = lax.ppermute(mine, "gy", core)
    return jnp.where(low, jnp.concatenate([mine, other]), jnp.concatenate([other, mine]))


def beside(block, axis, dim):
    count = lax.axis_size(axis)
    forward = [(i, i + 1) for i in range(count - 1)]
    backward = [(b, a) for a, b in forward]
    size = block[0].shape[dim]

    def face(at):
        return jnp.stack([lax.index_in_dim(b, at, dim, keepdims=False) for b in block])

    return (
        lax.ppermute(face(size - 1), axis, forward),
        lax.ppermute(face(0), axis, backward),
    )


def body(field, kappa, history):
    past = history.shape[0]
    x = beside((field, kappa), "gx", 0)
    y = beside((field, kappa), "gy", 1)
    h = history.reshape(past, -1, 128)
    g = gram(h)
    first, s1 = step(field, kappa, x, x, y, y)
    second, s2 = step(first, kappa, beside((first,), "gx", 0), x, beside((first,), "gy", 1), y)
    g = rows(h, s1, s2, g)
    count = h.shape[1] * 128 * lax.axis_size("gx") * lax.axis_size("gy")
    factor, inverse = chol(total(g) / count)
    s = jnp.stack([s1, s2]).reshape(2, -1, 128)
    out = basis(inverse, h, s)
    return second, out.reshape((out.shape[0],) + history.shape[1:]), factor


def solution(mesh):
    return jax.shard_map(
        body,
        mesh=mesh,
        in_specs=(P("gx", "gy", None), P("gx", "gy", None), P(None, "gx", "gy", None)),
        out_specs=(P("gx", "gy", None), P(None, "gx", "gy", None), P()),
        check_vma=False,
    )
```
